1024 devices in a mesh: cells: 32 (over y, x, core), region: 32 (over z).
Axes of the slice: x: 4, y: 4, z: 32, core: 2. Of those that a mesh axis runs over, the one named last changes fastest.
Arguments:
- cell_shape: bfloat16 [1024, 3, 544], P(('cells', 'region')), may hold values from -6 to 6
- upsample: bfloat16 [544, 2112], replicated, may hold values from -0.25 to 0.25
- bending: bfloat16 [544, 2112], replicated, may hold values from -0.25 to 0.25
- to_density: bfloat16 [2112, 152], replicated, may hold values from -0.125 to 0.125
- translate: bfloat16 [456, 456], replicated, may hold values from -0.25 to 0.25
- evaluate: bfloat16 [152, 2112], replicated, may hold values from -0.5 to 0.5
- smoothing: bfloat16 [2112, 544], replicated, may hold values from -0.125 to 0.125
- block_owner: int32 [270336, 1], P(('cells', 'region')), may hold values from 0 to 31; in each aligned block of 264 rows (0 to 263, 264 to 527, ...) at most 10 rows name the same one
- block_octant: int32 [270336], P(('cells', 'region')), may hold values from 0 to 63
- far_list: int32 [1024, 8], P(('cells', 'region')), may hold values from 0 to 2047
Outputs:
- velocity: float32 [1024, 3, 544], P(('cells', 'region'))
The draws below stay inside these ranges and needn't reach their ends.
Inputs may be any that keep to these rules, and one draw needn't show every extreme that they name: `block_owner`: among the 264 blocks of one device no owner is named more than 10 times, and in some device's blocks one owner is named exactly 10 times.
All inputs are finite; a program needn't handle non-finite values.
Results may differ from the reference program's by a relative error of at most 0.0063.
Values may be sent and summed in bfloat16 or wider, within the bound.
A program may use at most 32 MiB of HBM per device.

```python
import math
from functools import partial
import jax
import jax.numpy as jnp
import numpy as np
from jax import lax

P_COARSE = 544
P_FINE = 2112
EQ_PTS = 152
EQUIV = 456
BLK = 8
CELL_DEV = 1
NLIST = 8
OCT_DEV = 2
CELLS = 1024
NB = 264
BLOCKS = 270336
OWNERS = 32
MOST = 10
OCT_R = 64
OCTANTS = 2048
N_CELLS = 32
N_REGION = 32


def set_ends(drawn, stream_key, least, largest):
    place = [jax.random.randint(jax.random.fold_in(stream_key, axis), (), 0, length) for axis, length in enumerate(drawn.shape)]
    widest = drawn.shape.index(max(drawn.shape))
    neighbour = place[:widest] + [(place[widest] + 1) % drawn.shape[widest]] + place[widest + 1:]
    return drawn.at[tuple(place)].set(least).at[tuple(neighbour)].set(largest)


def block_levels(own_key, shape, pieces, low, top_value):
    gain = 1.0
    for axis_at, shards_of in pieces:
        steps = jax.random.uniform(jax.random.fold_in(jax.random.fold_in(own_key, 6), axis_at), (shards_of,), jnp.float32, low / len(pieces), top_value / len(pieces))
        gain = gain * jnp.repeat(jnp.exp(steps), shape[axis_at] // shards_of).reshape((-1,) + (1,) * (len(shape) - 1 - axis_at))
    return gain


def routed_block(own_key, own, number, rows, number_of, top, reach, lean):
    sequence = jax.random.permutation(own_key, number_of)
    heavy_load, common = portions_of(number_of, rows * top, reach, lean, True), portions_of(number_of, rows * top, reach, lean, False)
    places = jnp.arange(number_of)

    def named(sizes, rotation):
        used = int((sizes > 0).sum())
        fixed = max(1, used // 4)
        moved = fixed + (places - fixed + rotation * (used - fixed)) % max(1, number_of - fixed)
        return jnp.zeros((number_of,), jnp.int32).at[sequence[jnp.where(places < fixed, places, moved)]].set(jnp.asarray(sizes, jnp.int32))

    sizes = jnp.where(number % 4 == 0, named(heavy_load, number // 4), named(common, number - number // 4 - 1))
    mixed = jax.random.permutation(jax.random.fold_in(own, 3), number_of)
    source_of, receiver = mixed[0:number_of // 2 * 2:2], mixed[1:number_of // 2 * 2:2]
    margin = jnp.minimum(sizes[source_of] - 1, reach - sizes[receiver]) // 2
    margin = jnp.where((source_of == sequence[0]) | (receiver == sequence[0]) | (sizes[receiver] == 0), 0, jnp.maximum(margin, 0))
    moved = jax.random.randint(jax.random.fold_in(own, 4), (number_of // 2,), 0, 1 << 20) % (margin + 1)
    sizes = sizes.at[source_of].add(-moved).at[receiver].add(moved)
    labels = jnp.searchsorted(jnp.cumsum(sizes), jnp.arange(rows * top), side="right").astype(jnp.int32)
    table = labels.reshape(top, rows).T
    table = table[jax.random.permutation(jax.random.fold_in(own, 1), rows)]
    rotation = jax.random.randint(jax.random.fold_in(own, 2), (rows, 1), 0, top)
    return jnp.take_along_axis(table, (jnp.arange(top)[None, :] + rotation) % top, axis=1)


def portions_of(number_of, total, limit, skew, full):
    portions = [(1 << 20) // math.isqrt(standing ** skew) + 1 for standing in range(1, number_of + 1)]
    largest = limit if full else min(limit, max(-(-total // number_of), total * portions[0] // sum(portions)))
    least = 1 if total - largest >= number_of - 1 else 0
    given, rest = [largest] + [least] * (number_of - 1), total - largest - least * (number_of - 1)
    while rest > 0:
        movable = [i for i in range(1, number_of) if given[i] < largest] or [i for i in range(1, number_of) if given[i] < limit]
        pool, left = sum([portions[i] for i in movable]), rest
        for i in movable:
            more = min(limit - given[i], max(1, left * portions[i] // pool), rest)
            given[i] = given[i] + more
            rest = rest - more
    return np.array(given)


def noise(rng, extent, deviation, most, pieces=(), kind=jnp.bfloat16):
    factor_of = block_levels(rng, extent, pieces, -0.22, 0.18) if pieces else 1.0
    entries = jax.random.normal(rng, extent, jnp.float32) * deviation * factor_of
    return jnp.minimum(jnp.maximum(entries, -most), most).astype(kind)


def setup_inputs(seed: int = 0) -> dict:
    splits = jax.random.split(jax.random.key(seed), 11)
    cell_shape = noise(splits[0], (CELLS, 3, P_COARSE), 1.0, 6.0, ((0, 1024),))
    upsample = noise(splits[1], (P_COARSE, P_FINE), P_COARSE ** -0.5, 0.25)
    bending = noise(splits[2], (P_COARSE, P_FINE), P_COARSE ** -0.5, 0.25)
    to_density = noise(splits[3], (P_FINE, EQ_PTS), P_FINE ** -0.5, 0.125)
    translate = noise(splits[4], (EQUIV, EQUIV), EQUIV ** -0.5, 0.25)
    evaluate = noise(splits[5], (EQ_PTS, P_FINE), EQ_PTS ** -0.5, 0.5)
    smoothing = noise(splits[6], (P_FINE, P_COARSE), P_FINE ** -0.5, 0.125)
    block_owner_keys = jax.random.split(jax.random.fold_in(splits[7], 1), BLOCKS // NB)
    block_owner_turns = jax.random.permutation(jax.random.fold_in(splits[7], 3), BLOCKS // NB)
    block_owner = jax.vmap(lambda own, number: routed_block(jax.random.fold_in(splits[7], 2), own, number, NB, OWNERS, 1, MOST, 2))(block_owner_keys, block_owner_turns).reshape((BLOCKS, 1))
    block_octant = set_ends(jax.random.randint(splits[8], (BLOCKS,), 0, OCT_R), jax.random.fold_in(splits[8], 1), 0, OCT_R - 1).astype(jnp.int32)
    far_list = set_ends(jax.random.randint(splits[9], (CELLS, NLIST), 0, OCTANTS), jax.random.fold_in(splits[9], 1), 0, OCTANTS - 1).astype(jnp.int32)
    return {"cell_shape": cell_shape, "upsample": upsample, "bending": bending, "to_density": to_density, "translate": translate, "evaluate": evaluate, "smoothing": smoothing, "block_owner": block_owner, "block_octant": block_octant, "far_list": far_list}


EPSILON_SQ = 0.0625
STOKES_SCALE = 1.0 / (8.0 * 3.141592653589793)

def stokeslet(targets, sources, strength):
    diff_x = targets[0][:, None] - sources[0][None, :]
    diff_y = targets[1][:, None] - sources[1][None, :]
    diff_z = targets[2][:, None] - sources[2][None, :]
    radius_sq = diff_x * diff_x + diff_y * diff_y + diff_z * diff_z + EPSILON_SQ
    inverse = lax.rsqrt(radius_sq)
    cubed = inverse * inverse * inverse
    direct = (radius_sq + EPSILON_SQ) * cubed
    radial = (diff_x * strength[0][None, :] + diff_y * strength[1][None, :] + diff_z * strength[2][None, :]) * cubed
    vel_x = lax.optimization_barrier(jnp.sum(direct * strength[0][None, :] + diff_x * radial, axis=1))
    vel_y = lax.optimization_barrier(jnp.sum(direct * strength[1][None, :] + diff_y * radial, axis=1))
    vel_z = lax.optimization_barrier(jnp.sum(direct * strength[2][None, :] + diff_z * radial, axis=1))
    return jnp.stack([vel_x, vel_y, vel_z]) * STOKES_SCALE

def near_field(leaf_points):
    sources = leaf_points[:3].astype(jnp.float32)
    strength = leaf_points[3:].astype(jnp.float32)
    point_total = sources.shape[1]
    padding = -point_total % 256
    padded = jnp.pad(sources, ((0, 0), (0, padding)))
    tile_set = padded.reshape(3, -1, 256).transpose(1, 0, 2)
    result = lax.map(partial(stokeslet, sources=sources, strength=strength), tile_set)
    return result.transpose(1, 0, 2).reshape(3, -1)[:, :point_total]

def slot_numbers(owner, owners_count, capacity):
    onehot = (owner[:, None] == jnp.arange(owners_count, dtype=jnp.int32)[None, :]).astype(jnp.int32)
    before = jnp.cumsum(onehot, axis=0) - onehot
    slot_rank = lax.optimization_barrier(jnp.sum(before * onehot, axis=1))
    return (owner * capacity + slot_rank).astype(jnp.int32)

def place_blocks(block_data, slot_index, slot_total):
    empty = jnp.zeros((slot_total,) + block_data.shape[1:], block_data.dtype)
    return empty.at[slot_index].set(block_data)

def pick_blocks(returned, slot_index):
    return returned[slot_index]

def region_density(inputs_pair, to_density):
    region_forces, region_octant = inputs_pair
    octant_rows = OCT_DEV * N_CELLS
    choose = region_octant[None] == jnp.arange(octant_rows, dtype=jnp.int32)[:, None, None]
    masked = jnp.where(choose[:, :, None, :], region_forces[None], jnp.zeros((), region_forces.dtype))
    product = jnp.dot(masked.reshape(-1, P_FINE), to_density, preferred_element_type=jnp.float32)
    product = product.reshape(octant_rows, -1, 3 * EQ_PTS)
    return lax.optimization_barrier(jnp.sum(product, axis=1))

def reference(cell_shape, upsample, bending, to_density, translate, evaluate, smoothing, block_owner, block_octant, far_list):
    devices = N_CELLS * N_REGION
    per_cell = P_FINE // BLK
    block_count = CELL_DEV * per_cell
    capacity = block_count // N_CELLS + 2
    coarse = cell_shape.reshape(CELLS * 3, P_COARSE)
    points = jnp.dot(coarse, upsample, preferred_element_type=jnp.float32).astype(jnp.bfloat16).reshape(CELLS, 3, P_FINE)
    forces = jnp.dot(coarse, bending, preferred_element_type=jnp.float32).astype(jnp.bfloat16).reshape(CELLS, 3, P_FINE)
    stacked = jnp.concatenate([points, forces], axis=1)
    blocks = stacked.reshape(devices, CELL_DEV, 6, per_cell, BLK).transpose(0, 1, 3, 2, 4).reshape(devices, block_count, 6, BLK)
    owners = block_owner.reshape(devices, block_count)
    slot_index = jax.vmap(partial(slot_numbers, owners_count=N_CELLS, capacity=capacity))(owners)
    buffers = jax.vmap(partial(place_blocks, slot_total=N_CELLS * capacity))(blocks, slot_index)
    buffers = buffers.reshape(N_CELLS, N_REGION, N_CELLS, capacity, 6, BLK)
    leaves = buffers.transpose(1, 2, 4, 0, 3, 5).reshape(N_REGION * N_CELLS, 6, N_CELLS * capacity * BLK)
    near_vel = lax.map(near_field, leaves)
    near_vel = near_vel.reshape(N_REGION, N_CELLS, 3, N_CELLS, capacity, BLK).transpose(3, 0, 1, 4, 2, 5)
    near_vel = near_vel.reshape(devices, N_CELLS * capacity, 3, BLK)
    own_blocks = jax.vmap(pick_blocks)(near_vel, slot_index)
    near_points = own_blocks.reshape(devices, CELL_DEV, per_cell, 3, BLK).transpose(0, 1, 3, 2, 4).reshape(CELLS, 3, P_FINE)
    octant_blocks = block_octant.reshape(devices, CELL_DEV, per_cell, 1)
    point_octant = jnp.broadcast_to(octant_blocks, (devices, CELL_DEV, per_cell, BLK)).reshape(N_CELLS, N_REGION, CELL_DEV, P_FINE)
    region_forces = forces.reshape(N_CELLS, N_REGION, CELL_DEV, 3, P_FINE).transpose(1, 0, 2, 3, 4).reshape(N_REGION, N_CELLS * CELL_DEV, 3, P_FINE)
    region_octant = point_octant.transpose(1, 0, 2, 3).reshape(N_REGION, N_CELLS * CELL_DEV, P_FINE)
    density = lax.map(partial(region_density, to_density=to_density), (region_forces, region_octant))
    density_round = density.astype(jnp.bfloat16).reshape(-1, 3 * EQ_PTS)
    expansion = jnp.dot(density_round, translate, preferred_element_type=jnp.float32).astype(jnp.bfloat16)
    far_sum = lax.optimization_barrier(jnp.sum(expansion[far_list].astype(jnp.float32), axis=1))
    far_round = far_sum.astype(jnp.bfloat16).reshape(CELLS * 3, EQ_PTS)
    far_velocity = jnp.dot(far_round, evaluate, preferred_element_type=jnp.float32).reshape(CELLS, 3, P_FINE)
    total = (near_points + far_velocity).astype(jnp.bfloat16)
    velocity = jnp.dot(total.reshape(CELLS * 3, P_FINE), smoothing, preferred_element_type=jnp.float32)
    return velocity.reshape(CELLS, 3, P_COARSE)
```

```python
import jax
import jax.numpy as jnp
from jax import lax
from jax.experimental import pallas as pl
from jax.experimental.pallas import tpu as pltpu
from jax.sharding import PartitionSpec as P

P_COARSE = 544
P_FINE = 2112
EQ_PTS = 152
EQUIV = 456
NB = 264
NC = 32
NR = 32
SLOT = 16
CAP = 10
LEAF = NC * CAP * 8
NEAR = 4
TILE = 256
EPSILON_SQ = 0.0625
STOKES_SCALE = 1.0 / (8.0 * 3.141592653589793)

MESH = pl.DeviceIdType.MESH
F32 = jnp.float32
BF = jnp.bfloat16
I32 = jnp.int32


def iota(shape, axis):
    return lax.broadcasted_iota(I32, shape, axis)


def onehot(mask):
    return jnp.where(mask, 1.0, 0.0).astype(BF)


def dot(a, b):
    return jnp.dot(a, b, preferred_element_type=F32)


def dot_nt(a, b):
    return lax.dot_general(a, b, (((1,), (1,)), ((), ())), preferred_element_type=F32)


def pieces(value, count):
    found = []
    for at in range(count):
        part = value.astype(BF).astype(F32)
        found.append(part)
        if at + 1 < count:
            value = value - part
    return found


def spread_points(rows, lanes):
    keep = (iota((8, lanes), 1) & 7) == iota((8, lanes), 0)
    made = [jnp.where(keep, jnp.broadcast_to(row, (8, lanes)), 0.0) for row in rows]
    return jnp.concatenate(made, axis=0)


def gather_points(spread, lanes):
    keep = (iota((8, lanes), 1) & 7) == iota((8, lanes), 0)
    return [
        jnp.sum(jnp.where(keep, spread[8 * a : 8 * a + 8, :], 0.0), axis=0, keepdims=True)
        for a in range(spread.shape[0] // 8)
    ]


def kernel(
    cell_ref, owner_row_ref, owner_col_ref, octant_ref, far_ref,
    up_hbm, bend_hbm, td_hbm, tr_hbm, ev_hbm, sm_hbm,
    out_ref,
    up, bend, td, tr, ev, sm,
    expand, expand_leaf, place, masked,
    msg_d, msg_b, msg_r, msg_f, got_d, got_b, got_r, got_f, held,
    left_rows, right_rows, right_cols, weight_rows, weights, moments,
    counts, far_map, smooth_hi, smooth_lo,
    load_sem, sd, rd, sb, rb, sr, rr, sf, rf, sz, rz,
):
    me = lax.axis_index("cells")
    zr = lax.axis_index("region")

    def plus(k):
        return lax.rem(me + k, NC)

    def minus(k):
        return lax.rem(me + NC - k, NC)

    barrier = pltpu.get_barrier_semaphore()

    def greet(k, _):
        pl.semaphore_signal(barrier, inc=1, device_id=(plus(k), zr), device_id_type=MESH)
        return 0

    lax.fori_loop(1, NC, greet, 0)
    for d in range(1, NEAR + 1):
        for there in (lax.rem(zr + d, NR), lax.rem(zr + NR - d, NR)):
            pl.semaphore_signal(barrier, inc=1, device_id=(me, there), device_id_type=MESH)

    loads = [
        pltpu.make_async_copy(src, dst, load_sem.at[at])
        for at, (src, dst) in enumerate(
            ((bend_hbm, bend), (td_hbm, td), (up_hbm, up), (tr_hbm, tr), (ev_hbm, ev), (sm_hbm, sm))
        )
    ]
    for load in loads:
        load.start()

    def plane_copy(src, dst, send, recv, k, target):
        return pltpu.make_async_remote_copy(
            src_ref=src.at[k], dst_ref=dst.at[k], send_sem=send.at[k], recv_sem=recv.at[k],
            device_id=(target, zr), device_id_type=MESH,
        )

    def send_all(src, dst, send, recv, target_of):
        def step(k, _):
            plane_copy(src, dst, send, recv, k, target_of(k)).start()
            return 0

        lax.fori_loop(1, NC, step, 0)

    def recv_all(src, dst, send, recv, target_of):
        def step(k, _):
            plane_copy(src, dst, send, recv, k, target_of(k)).wait_recv()
            return 0

        lax.fori_loop(1, NC, step, 0)

    def sent_all(src, dst, send, recv, target_of):
        def step(k, _):
            plane_copy(src, dst, send, recv, k, target_of(k)).wait_send()
            return 0

        lax.fori_loop(1, NC, step, 0)

    expand[...] = onehot((iota((NB, P_FINE), 1) >> 3) == iota((NB, P_FINE), 0))
    octants = jnp.broadcast_to(octant_ref[...].astype(F32), (8, NB)).astype(BF)
    point_octant = dot(octants, expand[...])[0:1, :] - (2 * me).astype(F32)
    point_octant = jnp.where(point_octant < 0.0, point_octant + 2.0 * NC, point_octant)

    loads[0].wait()
    coarse = cell_ref[0]
    forces = dot(coarse, bend[...]).astype(BF).astype(F32)
    zero_row = jnp.zeros((1, P_FINE), F32)
    by_row = [forces[a // 2 : a // 2 + 1, :] for a in range(6)] + [zero_row, zero_row]
    by_row = jnp.concatenate(by_row + by_row, axis=0)
    sub = iota((16, P_FINE), 0)
    relative = jnp.broadcast_to(point_octant, (16, P_FINE)) - (2 * (sub >> 3) + (sub & 1)).astype(F32)
    for pair in range(NC // 2):
        masked[16 * pair : 16 * pair + 16, :] = jnp.where(relative == 4.0 * pair, by_row, 0.0).astype(BF)
    loads[1].wait()
    part = dot(masked[...], td[...])
    head = part[:, :128]
    tail = jnp.concatenate([part[:, 128:EQ_PTS], jnp.zeros((8 * NC, 256 - EQ_PTS), F32)], axis=1)
    row = iota((8 * NC, 128), 0) & 7
    lane = iota((8 * NC, 128), 1)
    joined = jnp.where(row < 6, head, 0.0)
    for comp in range(3):
        moved = pltpu.roll(tail, 6 - 2 * comp, axis=0)
        if comp:
            moved = pltpu.roll(moved, 24 * comp, axis=1)
        here = (row >= 6) & (lane >= 24 * comp) & (lane < 24 * comp + 24)
        joined = jnp.where(here, moved, joined)
    msg_d[...] = joined.reshape(NC, 8, 128).astype(BF)

    pl.semaphore_wait(barrier, NC - 1 + 2 * NEAR)
    send_all(msg_d, got_d, sd, rd, plus)
    got_d[0] = msg_d[0]

    owner = lax.rem(owner_row_ref[...] + (NC - me), NC)
    owner_col = lax.rem(owner_col_ref[...] + (NC - me), NC)
    same = (owner_col == owner) & (iota((NB, NB), 0) < iota((NB, NB), 1))
    rank = jnp.sum(jnp.where(same, 1.0, 0.0), axis=0, keepdims=True).astype(I32)
    slot = owner * SLOT + rank
    place[...] = onehot(iota((NC * SLOT, NB), 0) == slot)
    loads[2].wait()
    points = dot(coarse, up[...]).astype(BF).astype(F32)
    rows = [points[a : a + 1, :] for a in range(3)] + [forces[a : a + 1, :] for a in range(3)]
    by_block = dot_nt(spread_points(rows, P_FINE).astype(BF), expand[...])
    by_block = jnp.concatenate([by_block, jnp.zeros((80, NB), F32)], axis=0).astype(BF)
    listed = far_ref[...]
    lane = iota((1, 128), 1)
    far_row = jnp.zeros((1, 128), F32)
    for entry in range(8):
        number = listed[0:1, entry : entry + 1]
        far_row = jnp.where(lane == 64 + entry, (number >> 6).astype(F32), far_row)
        far_row = jnp.where(lane == 72 + entry, (number & 63).astype(F32), far_row)
    routed = dot_nt(place[...], by_block) + far_row
    msg_b[...] = routed.reshape(NC, SLOT, 128).astype(BF)
    send_all(msg_b, got_b, sb, rb, plus)
    got_b[0] = msg_b[0]

    for at in range(NC * SLOT // 64):
        place_row = iota((64, LEAF), 0) + 64 * at
        rank_of = place_row & (SLOT - 1)
        first = jnp.where(rank_of < CAP, (place_row >> 4) * CAP + rank_of, -1)
        expand_leaf[64 * at : 64 * at + 64, :] = onehot((iota((64, LEAF), 1) >> 3) == first)

    recv_all(msg_d, got_d, sd, rd, plus)
    held[0] = jnp.sum(got_d[...].astype(F32), axis=0).astype(BF)

    def z_copy(src, dst, count, at, there):
        return pltpu.make_async_remote_copy(
            src_ref=held.at[pl.ds(src, count)], dst_ref=held.at[pl.ds(dst, count)],
            send_sem=sz.at[at], recv_sem=rz.at[at], device_id=(me, there), device_id_type=MESH,
        )

    ahead, behind = lax.rem(zr + NEAR, NR), lax.rem(zr + NR - NEAR, NR)
    stages = [[]]
    for d in range(1, NEAR + 1):
        stages[0].append(z_copy(0, NR - d, 1, 2 * d - 2, lax.rem(zr + d, NR)))
        stages[0].append(z_copy(0, d, 1, 2 * d - 1, lax.rem(zr + NR - d, NR)))
    for s in range(1, 4):
        count = 4 if s < 3 else 3
        at = 2 * NEAR + 2 * (s - 1)
        stages.append(
            [z_copy(32 - 4 * s, 28 - 4 * s, 4, at, ahead), z_copy(4 * s - 3, 4 * s + 1, count, at + 1, behind)]
        )

    def z_start(s):
        for copy in stages[s]:
            copy.start()

    def z_next(s):
        for copy in stages[s]:
            copy.wait_recv()
        if s < 3:
            z_start(s + 1)

    z_start(0)

    recv_all(msg_b, got_b, sb, rb, plus)
    arrived = got_b[...].reshape(NC * SLOT, 128)
    unit = onehot(iota((128, 128), 0) == iota((128, 128), 1))
    arrived_rows = dot_nt(unit, arrived)[:48, :].astype(BF)
    x0, x1, x2, f0, f1, f2 = gather_points(dot(arrived_rows, expand_leaf[...]), LEAF)
    x, f = (x0, x1, x2), (f0, f1, f2)
    size = x0 * x0 + x1 * x1 + x2 * x2
    work = x0 * f0 + x1 * f1 + x2 * f2
    one = jnp.ones((1, LEAF), F32)
    left = list(x) + pieces(size + EPSILON_SQ, 3) + [one, one, one]
    right = [-2.0 * v for v in x] + [one, one, one] + pieces(size, 3)
    left_rows[...] = jnp.concatenate(left + [jnp.zeros((7, LEAF), F32)], axis=0).astype(BF)
    right_rows[0:16, :] = jnp.concatenate(right + [jnp.zeros((7, LEAF), F32)], axis=0)
    features = list(f) + pieces(work, 3)
    for a in range(3):
        for b in range(3):
            features += pieces(x[a] * f[b], 2)
    for b in range(3):
        features += pieces(size * f[b] + x[b] * work, 3)
    for at, feature in enumerate(features):
        weight_rows[at : at + 1, :] = feature
    weight_rows[33:48, :] = jnp.zeros((15, LEAF), F32)
    weights[...] = weight_rows[...].astype(BF)
    for at in range(LEAF // TILE):
        span = slice(TILE * at, TILE * at + TILE)
        right_cols[span, :] = jnp.transpose(right_rows[:, span]).astype(BF)

    def near_tile(at, _):
        span = pl.ds(pl.multiple_of(at * TILE, TILE), TILE)
        target = left_rows[:, span]
        total = jnp.zeros((48, TILE), F32)
        for source in range(LEAF // TILE):
            piece = slice(TILE * source, TILE * source + TILE)
            spread = jnp.maximum(dot(right_cols[piece, 0:16], target), EPSILON_SQ)
            inverse = lax.rsqrt(spread)
            cubed = (inverse * inverse * inverse).astype(BF)
            total = total + dot(weights[:, piece], cubed)
        moments[:, span] = total
        return 0

    lax.fori_loop(0, 4, near_tile, 0)
    z_next(0)
    lax.fori_loop(4, 10, near_tile, 0)
    z_next(1)

    def moment(at, count=1):
        total = moments[at : at + 1, :]
        for more in range(1, count):
            total = total + moments[at + more : at + more + 1, :]
        return total

    plain = [moment(b) for b in range(3)]
    work_sum = moment(3, 3)
    cross = [[moment(6 + 2 * (3 * a + b), 2) for b in range(3)] for a in range(3)]
    high = [moment(24 + 3 * b, 3) for b in range(3)]
    along = x0 * plain[0] + x1 * plain[1] + x2 * plain[2] - work_sum
    near_hi, near_lo = [], []
    for b in range(3):
        value = (size + 2.0 * EPSILON_SQ) * plain[b] + high[b] + x[b] * along
        for a in range(3):
            value = value - x[a] * (2.0 * cross[a][b] + cross[b][a])
        hi, lo = pieces(value * STOKES_SCALE, 2)
        near_hi.append(hi)
        near_lo.append(lo)
    replies = spread_points(near_hi + near_lo, LEAF)
    replies = jnp.concatenate([replies, jnp.zeros((80, LEAF), F32)], axis=0).astype(BF)
    msg_r[...] = dot_nt(expand_leaf[...], replies).reshape(NC, SLOT, 128).astype(BF)
    send_all(msg_r, got_r, sr, rr, minus)
    got_r[0] = msg_r[0]

    for load in loads[3:]:
        load.wait()
    spot, width = iota((512, EQUIV), 0), iota((512, EQUIV), 1)
    group, inner = spot >> 7, spot & 127
    third = jnp.where(inner < 24, 0, jnp.where(inner < 48, 1, 2))
    flat = jnp.where(group < 3, group * EQ_PTS + inner, third * EQ_PTS + 128 + inner - 24 * third)
    flat = jnp.where((group == 3) & (inner >= 72), -1, flat)
    ordered = dot(onehot(flat == width), tr[...]).astype(BF)
    entry, column = iota((EQUIV, 768), 0), iota((EQUIV, 768), 1)
    wanted = (column >> 8) * EQ_PTS + (column & 255)
    far_map[...] = dot(ordered, onehot((entry == wanted) & ((column & 255) < EQ_PTS))).astype(BF)
    smooth = dot(ev[...], sm[...])
    smooth_hi[0:EQ_PTS, :] = smooth.astype(BF)
    smooth_lo[0:EQ_PTS, :] = (smooth - smooth.astype(BF).astype(F32)).astype(BF)
    z_next(2)

    keys = got_b[...].astype(F32)[:, 0:8, :].reshape(8 * NC, 128)
    column = iota((1, 8 * NR), 1)
    held_key = (lax.rem((column >> 3) + zr, NR) * 64 + 2 * me + (column & 1)).astype(F32)
    total = jnp.zeros((8 * NC, 8 * NR), F32)
    for entry in range(8):
        key = keys[:, 64 + entry : 65 + entry] * 64.0 + keys[:, 72 + entry : 73 + entry]
        total = total + jnp.where(key == held_key, 1.0, 0.0)
    shape = (8 * NC, 8 * NR)
    fits = ((iota(shape, 1) & 7) >> 1) == (iota(shape, 0) & 7)
    counts[...] = jnp.where(fits, total, 0.0).astype(BF)

    recv_all(msg_r, got_r, sr, rr, minus)
    returned = got_r[...].reshape(NC * SLOT, 128)
    returned_rows = dot_nt(unit, returned)[:48, :].astype(BF)
    own = dot(returned_rows, place[...]).astype(BF)
    near = gather_points(dot(own, expand[...]), P_FINE)
    near = [near[b] + near[3 + b] for b in range(3)]
    near = jnp.concatenate(near + [jnp.zeros((5, P_FINE), F32)], axis=0).astype(BF)
    velocity = dot(near, sm[...])

    z_next(3)
    octant_rows = held[...].astype(F32).reshape(8 * NR, 128).astype(BF)
    msg_f[...] = dot(counts[...], octant_rows).reshape(NC, 8, 128).astype(BF)
    send_all(msg_f, got_f, sf, rf, minus)
    got_f[0] = msg_f[0]
    recv_all(msg_f, got_f, sf, rf, minus)
    summed = jnp.sum(got_f[...].astype(F32), axis=0)
    turn = iota((8, 128), 0)
    line = jnp.concatenate([jnp.where(turn == g, summed, 0.0) for g in range(4)], axis=1)
    hi, lo = pieces(line, 2)
    moved = dot(jnp.concatenate([hi, lo], axis=0).astype(BF), far_map[...])
    moved = jnp.sum(moved, axis=0, keepdims=True)
    far = [moved[:, 256 * b : 256 * b + EQ_PTS] for b in range(3)]
    far = jnp.concatenate(far + [jnp.zeros((5, EQ_PTS), F32)], axis=0).astype(BF)
    velocity = velocity + dot(far, smooth_hi[...]) + dot(far, smooth_lo[...])
    out_ref[0] = velocity[0:3, :]

    sent_all(msg_d, got_d, sd, rd, plus)
    sent_all(msg_b, got_b, sb, rb, plus)
    sent_all(msg_r, got_r, sr, rr, minus)
    sent_all(msg_f, got_f, sf, rf, minus)
    for stage in stages:
        for copy in stage:
            copy.wait_send()


def on_device(
    cell_shape, upsample, bending, to_density, translate, evaluate, smoothing,
    block_owner, block_octant, far_list,
):
    vmem = pl.BlockSpec(memory_space=pltpu.VMEM)
    anywhere = pl.BlockSpec(memory_space=pl.ANY)
    owner_row = block_owner.reshape(1, NB)
    octant = block_octant.reshape(1, NB)
    dma = pltpu.SemaphoreType.DMA
    return pl.pallas_call(
        kernel,
        out_shape=jax.ShapeDtypeStruct((1, 3, P_COARSE), F32),
        in_specs=[vmem] * 5 + [anywhere] * 6,
        out_specs=vmem,
        scratch_shapes=[
            pltpu.VMEM((P_COARSE, P_FINE), BF),
            pltpu.VMEM((P_COARSE, P_FINE), BF),
            pltpu.VMEM((P_FINE, EQ_PTS), BF),
            pltpu.VMEM((EQUIV, EQUIV), BF),
            pltpu.VMEM((EQ_PTS, P_FINE), BF),
            pltpu.VMEM((P_FINE, P_COARSE), BF),
            pltpu.VMEM((NB, P_FINE), BF),
            pltpu.VMEM((NC * SLOT, LEAF), BF),
            pltpu.VMEM((NC * SLOT, NB), BF),
            pltpu.VMEM((8 * NC, P_FINE), BF),
            pltpu.VMEM((NC, 8, 128), BF),
            pltpu.VMEM((NC, SLOT, 128), BF),
            pltpu.VMEM((NC, SLOT, 128), BF),
            pltpu.VMEM((NC, 8, 128), BF),
            pltpu.VMEM((NC, 8, 128), BF),
            pltpu.VMEM((NC, SLOT, 128), BF),
            pltpu.VMEM((NC, SLOT, 128), BF),
            pltpu.VMEM((NC, 8, 128), BF),
            pltpu.VMEM((NR, 8, 128), BF),
            pltpu.VMEM((16, LEAF), BF),
            pltpu.VMEM((128, LEAF), F32),
            pltpu.VMEM((LEAF, 128), BF),
            pltpu.VMEM((48, LEAF), F32),
            pltpu.VMEM((48, LEAF), BF),
            pltpu.VMEM((48, LEAF), F32),
            pltpu.VMEM((8 * NC, 8 * NR), BF),
            pltpu.VMEM((512, 768), BF),
            pltpu.VMEM((EQ_PTS, P_COARSE), BF),
            pltpu.VMEM((EQ_PTS, P_COARSE), BF),
            dma((6,)),
        ]
        + [dma((NC,))] * 8
        + [dma((14,))] * 2,
        compiler_params=pltpu.CompilerParams(
            collective_id=0, has_side_effects=True, vmem_limit_bytes=60 * 1024 * 1024
        ),
    )(cell_shape, owner_row, block_owner, octant, far_list,
      upsample, bending, to_density, translate, evaluate, smoothing)


def solution(mesh):
    split = ("cells", "region")
    return jax.shard_map(
        on_device,
        mesh=mesh,
        in_specs=(
            P(split, None, None), P(), P(), P(), P(), P(), P(),
            P(split, None), P(split), P(split, None),
        ),
        out_specs=P(split, None, None),
        check_vma=False,
    )
```

```python
import jax
import jax.numpy as jnp
from jax import lax
from jax.experimental import pallas as pl
from jax.experimental.pallas import tpu as pltpu
from jax.sharding import PartitionSpec as P

P_COARSE = 544
P_FINE = 2112
EQ_PTS = 152
EQUIV = 456
NB = 264
NC = 32
NR = 32
SLOT = 16
CAP = 10
LEAF = NC * CAP * 8
NEAR = 4
TILE = 256
EPSILON_SQ = 0.0625
STOKES_SCALE = 1.0 / (8.0 * 3.141592653589793)

MESH = pl.DeviceIdType.MESH
F32 = jnp.float32
BF = jnp.bfloat16
I32 = jnp.int32


def iota(shape, axis):
    return lax.broadcasted_iota(I32, shape, axis)


def onehot(mask):
    return jnp.where(mask, 1.0, 0.0).astype(BF)


def dot(a, b):
    return jnp.dot(a, b, preferred_element_type=F32)


def dot_nt(a, b):
    return lax.dot_general(a, b, (((1,), (1,)), ((), ())), preferred_element_type=F32)


def pieces(value, count):
    found = []
    for at in range(count):
        part = value.astype(BF).astype(F32)
        found.append(part)
        if at + 1 < count:
            value = value - part
    return found


def spread_points(rows, lanes):
    keep = (iota((8, lanes), 1) & 7) == iota((8, lanes), 0)
    made = [jnp.where(keep, jnp.broadcast_to(row, (8, lanes)), 0.0) for row in rows]
    return jnp.concatenate(made, axis=0)


def gather_points(spread, lanes):
    keep = (iota((8, lanes), 1) & 7) == iota((8, lanes), 0)
    return [
        jnp.sum(jnp.where(keep, spread[8 * a : 8 * a + 8, :], 0.0), axis=0, keepdims=True)
        for a in range(spread.shape[0] // 8)
    ]


def kernel(
    cell_ref, owner_ref, octant_ref, far_ref,
    up_hbm, bend_hbm, td_hbm, tr_hbm, ev_hbm, sm_hbm,
    out_ref,
    up, bend, td, tr, ev, sm,
    expand, expand_leaf, place, masked,
    msg_d, msg_b, msg_r, msg_f, got_d, got_b, got_r, got_f, held,
    left_rows, right_rows, right_cols, weight_rows, weights, moments,
    counts, far_map, smooth_hi, smooth_lo,
    load_sem, sd, rd, sb, rb, sr, rr, sf, rf, sz, rz,
):
    me = lax.axis_index("cells")
    zr = lax.axis_index("region")

    def plus(k):
        return lax.rem(me + k, NC)

    def minus(k):
        return lax.rem(me + NC - k, NC)

    loads = [
        pltpu.make_async_copy(src, dst, load_sem.at[at])
        for at, (src, dst) in enumerate(
            ((bend_hbm, bend), (td_hbm, td), (up_hbm, up), (tr_hbm, tr), (ev_hbm, ev), (sm_hbm, sm))
        )
    ]
    loads[0].start()
    loads[1].start()

    barrier = pltpu.get_barrier_semaphore()

    def greet(k, _):
        pl.semaphore_signal(barrier, inc=1, device_id=(plus(k), zr), device_id_type=MESH)
        return 0

    lax.fori_loop(1, NC, greet, 0)
    for d in range(1, NEAR + 1):
        for there in (lax.rem(zr + d, NR), lax.rem(zr + NR - d, NR)):
            pl.semaphore_signal(barrier, inc=1, device_id=(me, there), device_id_type=MESH)

    def plane_copy(src, dst, send, recv, k, target):
        return pltpu.make_async_remote_copy(
            src_ref=src.at[k], dst_ref=dst.at[k], send_sem=send.at[k], recv_sem=recv.at[k],
            device_id=(target, zr), device_id_type=MESH,
        )

    def send_all(src, dst, send, recv, target_of):
        def step(k, _):
            plane_copy(src, dst, send, recv, k, target_of(k)).start()
            return 0

        lax.fori_loop(1, NC, step, 0)

    def recv_all(src, dst, send, recv, target_of):
        def step(k, _):
            plane_copy(src, dst, send, recv, k, target_of(k)).wait_recv()
            return 0

        lax.fori_loop(1, NC, step, 0)

    def sent_all(src, dst, send, recv, target_of):
        def step(k, _):
            plane_copy(src, dst, send, recv, k, target_of(k)).wait_send()
            return 0

        lax.fori_loop(1, NC, step, 0)

    expand[...] = onehot((iota((NB, P_FINE), 1) >> 3) == iota((NB, P_FINE), 0))
    octants = jnp.broadcast_to(octant_ref[...].reshape(1, NB).astype(F32), (8, NB)).astype(BF)
    point_octant = dot(octants, expand[...])[0:1, :] - (2 * me).astype(F32)
    point_octant = jnp.where(point_octant < 0.0, point_octant + 2.0 * NC, point_octant)

    loads[0].wait()
    loads[2].start()
    coarse = cell_ref[0]
    forces = dot(coarse, bend[...]).astype(BF).astype(F32)
    zero_row = jnp.zeros((1, P_FINE), F32)
    by_row = [forces[a // 2 : a // 2 + 1, :] for a in range(6)] + [zero_row, zero_row]
    by_row = jnp.concatenate(by_row + by_row, axis=0)
    sub = iota((16, P_FINE), 0)
    relative = jnp.broadcast_to(point_octant, (16, P_FINE)) - (2 * (sub >> 3) + (sub & 1)).astype(F32)
    for pair in range(NC // 2):
        masked[16 * pair : 16 * pair + 16, :] = jnp.where(relative == 4.0 * pair, by_row, 0.0).astype(BF)
    loads[1].wait()
    part = dot_nt(masked[...], td[...])
    head = part[:, :128]
    tail = jnp.concatenate([part[:, 128:EQ_PTS], jnp.zeros((8 * NC, 256 - EQ_PTS), F32)], axis=1)
    row = iota((8 * NC, 128), 0) & 7
    lane = iota((8 * NC, 128), 1)
    joined = jnp.where(row < 6, head, 0.0)
    for comp in range(3):
        moved = pltpu.roll(tail, 6 - 2 * comp, axis=0)
        if comp:
            moved = pltpu.roll(moved, 24 * comp, axis=1)
        here = (row >= 6) & (lane >= 24 * comp) & (lane < 24 * comp + 24)
        joined = jnp.where(here, moved, joined)
    msg_d[...] = joined.reshape(NC, 8, 128).astype(BF)

    pl.semaphore_wait(barrier, NC - 1 + 2 * NEAR)
    send_all(msg_d, got_d, sd, rd, plus)
    got_d[0] = msg_d[0]

    owner = lax.rem(owner_ref[...] + (NC - me), NC)
    mine = jnp.where(iota((NC, NB), 0) == owner, 1.0, 0.0)
    ahead_of = dot(mine.astype(BF), onehot(iota((NB, NB), 0) < iota((NB, NB), 1)))
    rank = jnp.sum(mine * ahead_of, axis=0, keepdims=True).astype(I32)
    slot = owner * SLOT + rank
    place[...] = onehot(iota((NC * SLOT, NB), 0) == slot)
    loads[2].wait()
    for load in loads[3:]:
        load.start()
    points = dot(coarse, up[...]).astype(BF).astype(F32)
    rows = [points[a : a + 1, :] for a in range(3)] + [forces[a : a + 1, :] for a in range(3)]
    by_block = dot_nt(spread_points(rows, P_FINE).astype(BF), expand[...])
    by_block = jnp.concatenate([by_block, jnp.zeros((80, NB), F32)], axis=0).astype(BF)
    listed = far_ref[...]
    lane = iota((1, 128), 1)
    far_row = jnp.zeros((1, 128), F32)
    for entry in range(8):
        number = listed[0:1, entry : entry + 1]
        far_row = jnp.where(lane == 64 + entry, (number >> 6).astype(F32), far_row)
        far_row = jnp.where(lane == 72 + entry, (number & 63).astype(F32), far_row)
    routed = dot_nt(place[...], by_block) + far_row
    msg_b[...] = routed.reshape(NC, SLOT, 128).astype(BF)
    send_all(msg_b, got_b, sb, rb, plus)
    got_b[0] = msg_b[0]

    for at in range(NC * SLOT // 64):
        place_row = iota((64, LEAF), 0) + 64 * at
        rank_of = place_row & (SLOT - 1)
        first = jnp.where(rank_of < CAP, (place_row >> 4) * CAP + rank_of, -1)
        expand_leaf[64 * at : 64 * at + 64, :] = onehot((iota((64, LEAF), 1) >> 3) == first)

    recv_all(msg_d, got_d, sd, rd, plus)
    held[0] = jnp.sum(got_d[...].astype(F32), axis=0).astype(BF)

    def z_copy(src, dst, count, at, there):
        return pltpu.make_async_remote_copy(
            src_ref=held.at[pl.ds(src, count)], dst_ref=held.at[pl.ds(dst, count)],
            send_sem=sz.at[at], recv_sem=rz.at[at], device_id=(me, there), device_id_type=MESH,
        )

    ahead, behind = lax.rem(zr + NEAR, NR), lax.rem(zr + NR - NEAR, NR)
    stages = [[]]
    for d in range(1, NEAR + 1):
        stages[0].append(z_copy(0, NR - d, 1, 2 * d - 2, lax.rem(zr + d, NR)))
        stages[0].append(z_copy(0, d, 1, 2 * d - 1, lax.rem(zr + NR - d, NR)))
    for s in range(1, 4):
        count = 4 if s < 3 else 3
        at = 2 * NEAR + 2 * (s - 1)
        stages.append(
            [z_copy(32 - 4 * s, 28 - 4 * s, 4, at, ahead), z_copy(4 * s - 3, 4 * s + 1, count, at + 1, behind)]
        )

    def z_start(s):
        for copy in stages[s]:
            copy.start()

    def z_next(s):
        for copy in stages[s]:
            copy.wait_recv()
        if s < 3:
            z_start(s + 1)

    z_start(0)

    recv_all(msg_b, got_b, sb, rb, plus)
    arrived = got_b[...].reshape(NC * SLOT, 128)
    unit = onehot(iota((128, 128), 0) == iota((128, 128), 1))
    arrived_rows = dot_nt(unit, arrived)[:48, :].astype(BF)
    x0, x1, x2, f0, f1, f2 = gather_points(dot(arrived_rows, expand_leaf[...]), LEAF)
    x, f = (x0, x1, x2), (f0, f1, f2)
    size = x0 * x0 + x1 * x1 + x2 * x2
    work = x0 * f0 + x1 * f1 + x2 * f2
    one = jnp.ones((1, LEAF), F32)
    left = list(x) + pieces(size + EPSILON_SQ, 3) + [one, one, one]
    right = [-2.0 * v for v in x] + [one, one, one] + pieces(size, 3)
    left_rows[...] = jnp.concatenate(left + [jnp.zeros((7, LEAF), F32)], axis=0).astype(BF)
    right_rows[0:16, :] = jnp.concatenate(right + [jnp.zeros((7, LEAF), F32)], axis=0)
    features = list(f) + pieces(work, 3)
    for a in range(3):
        for b in range(3):
            features += pieces(x[a] * f[b], 2)
    for b in range(3):
        features += pieces(size * f[b] + x[b] * work, 3)
    for at, feature in enumerate(features):
        weight_rows[at : at + 1, :] = feature
    weight_rows[33:48, :] = jnp.zeros((15, LEAF), F32)
    weights[...] = weight_rows[...].astype(BF)
    for at in range(LEAF // TILE):
        span = slice(TILE * at, TILE * at + TILE)
        right_cols[span, :] = jnp.transpose(right_rows[:, span]).astype(BF)

    def near_tile(at, _):
        span = pl.ds(pl.multiple_of(at * TILE, TILE), TILE)
        target = left_rows[:, span]
        total = jnp.zeros((48, TILE), F32)
        for source in range(LEAF // TILE):
            piece = slice(TILE * source, TILE * source + TILE)
            spread = jnp.maximum(dot(right_cols[piece, 0:16], target), EPSILON_SQ)
            inverse = lax.rsqrt(spread)
            cubed = (inverse * inverse * inverse).astype(BF)
            total = total + dot(weights[:, piece], cubed)
        moments[:, span] = total
        return 0

    done = 0
    for stage, upto in enumerate((1, 5, 9)):
        lax.fori_loop(done, upto, near_tile, 0)
        z_next(stage)
        done = upto
    lax.fori_loop(done, LEAF // TILE, near_tile, 0)

    def moment(at, count=1):
        total = moments[at : at + 1, :]
        for more in range(1, count):
            total = total + moments[at + more : at + more + 1, :]
        return total

    plain = [moment(b) for b in range(3)]
    work_sum = moment(3, 3)
    cross = [[moment(6 + 2 * (3 * a + b), 2) for b in range(3)] for a in range(3)]
    high = [moment(24 + 3 * b, 3) for b in range(3)]
    along = x0 * plain[0] + x1 * plain[1] + x2 * plain[2] - work_sum
    near_hi, near_lo = [], []
    for b in range(3):
        value = (size + 2.0 * EPSILON_SQ) * plain[b] + high[b] + x[b] * along
        for a in range(3):
            value = value - x[a] * (2.0 * cross[a][b] + cross[b][a])
        hi, lo = pieces(value * STOKES_SCALE, 2)
        near_hi.append(hi)
        near_lo.append(lo)
    replies = spread_points(near_hi + near_lo, LEAF)
    replies = jnp.concatenate([replies, jnp.zeros((80, LEAF), F32)], axis=0).astype(BF)
    msg_r[...] = dot_nt(expand_leaf[...], replies).reshape(NC, SLOT, 128).astype(BF)
    send_all(msg_r, got_r, sr, rr, minus)
    got_r[0] = msg_r[0]

    keys = got_b[...].astype(F32)[:, 0:8, :].reshape(8 * NC, 128)
    column = iota((1, 8 * NR), 1)
    held_key = (lax.rem((column >> 3) + zr, NR) * 64 + 2 * me + (column & 1)).astype(F32)
    total = jnp.zeros((8 * NC, 8 * NR), F32)
    for entry in range(8):
        key = keys[:, 64 + entry : 65 + entry] * 64.0 + keys[:, 72 + entry : 73 + entry]
        total = total + jnp.where(key == held_key, 1.0, 0.0)
    shape = (8 * NC, 8 * NR)
    fits = ((iota(shape, 1) & 7) >> 1) == (iota(shape, 0) & 7)
    counts[...] = jnp.where(fits, total, 0.0).astype(BF)

    for load in loads[3:]:
        load.wait()
    spot, width = iota((512, EQUIV), 0), iota((512, EQUIV), 1)
    group, inner = spot >> 7, spot & 127
    third = jnp.where(inner < 24, 0, jnp.where(inner < 48, 1, 2))
    flat = jnp.where(group < 3, group * EQ_PTS + inner, third * EQ_PTS + 128 + inner - 24 * third)
    flat = jnp.where((group == 3) & (inner >= 72), -1, flat)
    ordered = dot(onehot(flat == width), tr[...]).astype(BF)
    entry, column = iota((EQUIV, 768), 0), iota((EQUIV, 768), 1)
    wanted = (column >> 8) * EQ_PTS + (column & 255)
    far_map[...] = dot(ordered, onehot((entry == wanted) & ((column & 255) < EQ_PTS))).astype(BF)
    smooth = dot_nt(ev[...], sm[...])
    smooth_hi[0:EQ_PTS, :] = smooth.astype(BF)
    smooth_lo[0:EQ_PTS, :] = (smooth - smooth.astype(BF).astype(F32)).astype(BF)
    z_next(3)
    octant_rows = held[...].astype(F32).reshape(8 * NR, 128).astype(BF)
    msg_f[...] = dot(counts[...], octant_rows).reshape(NC, 8, 128).astype(BF)
    send_all(msg_f, got_f, sf, rf, minus)
    got_f[0] = msg_f[0]

    sent_all(msg_d, got_d, sd, rd, plus)
    sent_all(msg_b, got_b, sb, rb, plus)
    sent_all(msg_r, got_r, sr, rr, minus)
    for stage in stages:
        for copy in stage:
            copy.wait_send()

    recv_all(msg_r, got_r, sr, rr, minus)
    returned = got_r[...].reshape(NC * SLOT, 128)
    returned_rows = dot_nt(unit, returned)[:48, :].astype(BF)
    own = dot(returned_rows, place[...]).astype(BF)
    near = gather_points(dot(own, expand[...]), P_FINE)
    near = [near[b] + near[3 + b] for b in range(3)]
    near = jnp.concatenate(near + [jnp.zeros((5, P_FINE), F32)], axis=0).astype(BF)
    velocity = dot_nt(near, sm[...])

    recv_all(msg_f, got_f, sf, rf, minus)
    summed = jnp.sum(got_f[...].astype(F32), axis=0)
    turn = iota((8, 128), 0)
    line = jnp.concatenate([jnp.where(turn == g, summed, 0.0) for g in range(4)], axis=1)
    hi, lo = pieces(line, 2)
    moved = dot(jnp.concatenate([hi, lo], axis=0).astype(BF), far_map[...])
    moved = jnp.sum(moved, axis=0, keepdims=True)
    far = [moved[:, 256 * b : 256 * b + EQ_PTS] for b in range(3)]
    far = jnp.concatenate(far + [jnp.zeros((5, EQ_PTS), F32)], axis=0).astype(BF)
    velocity = velocity + dot(far, smooth_hi[...]) + dot(far, smooth_lo[...])
    for comp in range(3):
        out_ref[comp] = velocity[comp : comp + 1, :]

    sent_all(msg_f, got_f, sf, rf, minus)


def on_device(
    cell_shape, upsample, bending, to_density, translate, evaluate, smoothing,
    block_owner, block_octant, far_list,
):
    vmem = pl.BlockSpec(memory_space=pltpu.VMEM)
    anywhere = pl.BlockSpec(memory_space=pl.ANY)
    dma = pltpu.SemaphoreType.DMA
    made = pl.pallas_call(
        kernel,
        out_shape=jax.ShapeDtypeStruct((3, 1, P_COARSE), F32),
        in_specs=[vmem] * 4 + [anywhere] * 6,
        out_specs=vmem,
        scratch_shapes=[
            pltpu.VMEM((P_COARSE, P_FINE), BF),
            pltpu.VMEM((P_COARSE, P_FINE), BF),
            pltpu.VMEM((EQ_PTS, P_FINE), BF),
            pltpu.VMEM((EQUIV, EQUIV), BF),
            pltpu.VMEM((EQ_PTS, P_FINE), BF),
            pltpu.VMEM((P_COARSE, P_FINE), BF),
            pltpu.VMEM((NB, P_FINE), BF),
            pltpu.VMEM((NC * SLOT, LEAF), BF),
            pltpu.VMEM((NC * SLOT, NB), BF),
            pltpu.VMEM((8 * NC, P_FINE), BF),
            pltpu.VMEM((NC, 8, 128), BF),
            pltpu.VMEM((NC, SLOT, 128), BF),
            pltpu.VMEM((NC, SLOT, 128), BF),
            pltpu.VMEM((NC, 8, 128), BF),
            pltpu.VMEM((NC, 8, 128), BF),
            pltpu.VMEM((NC, SLOT, 128), BF),
            pltpu.VMEM((NC, SLOT, 128), BF),
            pltpu.VMEM((NC, 8, 128), BF),
            pltpu.VMEM((NR, 8, 128), BF),
            pltpu.VMEM((16, LEAF), BF),
            pltpu.VMEM((128, LEAF), F32),
            pltpu.VMEM((LEAF, 128), BF),
            pltpu.VMEM((48, LEAF), F32),
            pltpu.VMEM((48, LEAF), BF),
            pltpu.VMEM((48, LEAF), F32),
            pltpu.VMEM((8 * NC, 8 * NR), BF),
            pltpu.VMEM((512, 768), BF),
            pltpu.VMEM((EQ_PTS, P_COARSE), BF),
            pltpu.VMEM((EQ_PTS, P_COARSE), BF),
            dma((6,)),
        ]
        + [dma((NC,))] * 8
        + [dma((14,))] * 2,
        compiler_params=pltpu.CompilerParams(
            collective_id=0, has_side_effects=True, vmem_limit_bytes=60 * 1024 * 1024
        ),
    )(cell_shape, block_owner.reshape(1, NB), block_octant, far_list,
      upsample, bending, to_density.T, translate, evaluate, smoothing.T)
    return jnp.transpose(made, (1, 0, 2))


def solution(mesh):
    split = ("cells", "region")
    return jax.shard_map(
        on_device,
        mesh=mesh,
        in_specs=(
            P(split, None, None), P(), P(), P(), P(), P(), P(),
            P(split, None), P(split), P(split, None),
        ),
        out_specs=P(split, None, None),
        check_vma=False,
    )
```
